768 devices in a mesh: row: 192 (over z, y, core), col: 4 (over x).
Axes of the slice: x: 4, y: 8, z: 12, core: 2. Of those that a mesh axis runs over, the one named last changes fastest.
Arguments:
- fine_matrix: bfloat16 [49152, 1536], P('row', 'col'), may hold values from -0.75 to 0.75
- fine_columns: int32 [768, 24], P('row'), may hold values from 0 to 767, as said below
- fine_counts: int32 [768], P('row'), may hold values from 12 to 24, as said below
- prolong: bfloat16 [49152, 128], P('row'), may hold values from -6 to 6
- prolong_columns: int32 [768, 2], P('row'), may hold values from 0 to 383
- restrict_rows: bfloat16 [24576, 256], P('row'), may hold values from -0.375 to 0.375
- coarse_pattern: int32 [192, 48], P('row'), may hold values from -1 to 383, as said below
Outputs:
- coarse_operator: float32 [24576, 3072], P('row', 'col')
The draws below stay inside these ranges and needn't reach their ends.
Inputs may be any that keep to these rules, and one draw needn't show every extreme that they name: Only the first fine_counts[i] block slots of fine brick i are live. `fine_columns`: at most 4 block slots of each fine brick couple to a brick more than 8 bricks away, counting cyclically over the 768 bricks. `coarse_pattern`: each row holds distinct coarse brick numbers and -1 in slots left empty; every coarse brick reached by a live product of the slab is listed.
All inputs are finite; a program needn't handle non-finite values.
Results may differ from the reference program's by a relative error of at most 0.00035.
Values may be sent and summed in bfloat16 or wider, within the bound.
A program may use at most 32 MiB of HBM per device.

```python
import jax
import jax.numpy as jnp
from jax import lax

BRICK = 64
SLAB_BRICKS = 4
A_SLOTS = 24
P_SLOTS = 2
NEAR = 8
FAR_SLOTS = 4
SLABS = 192
FINE = 768
COARSE = 384
PATTERN = 48
PATTERN_OWN = 12


def layout(key):
    near_key = jax.random.fold_in(key, 11)
    far_key = jax.random.fold_in(key, 23)
    order_key = jax.random.fold_in(key, 37)
    count_key = jax.random.fold_in(key, 41)
    side_key = jax.random.fold_in(key, 53)
    rows = jnp.arange(FINE, dtype=jnp.int32)
    offsets = jax.random.randint(near_key, (FINE, A_SLOTS), -NEAR, NEAR + 1, dtype=jnp.int32)
    distant = jax.random.randint(far_key, (FINE, A_SLOTS), 0, FINE, dtype=jnp.int32)
    scores = jax.random.randint(order_key, (FINE, A_SLOTS), 0, 1 << 20, dtype=jnp.int32) * A_SLOTS
    scores = scores + jnp.arange(A_SLOTS, dtype=jnp.int32)[None, :]
    ranks = jnp.argsort(jnp.argsort(scores, axis=1), axis=1)
    columns = jnp.where(ranks < FAR_SLOTS, distant, (rows[:, None] + offsets) % FINE).astype(jnp.int32)
    counts = jax.random.randint(count_key, (FINE,), A_SLOTS // 2, A_SLOTS + 1, dtype=jnp.int32)
    counts = counts.at[0].set(A_SLOTS)
    side = jax.random.randint(side_key, (FINE,), 0, 2, dtype=jnp.int32) * 2 - 1
    parent = rows // 2
    targets = jnp.stack([parent, (parent + side) % COARSE], axis=1).astype(jnp.int32)
    reached = targets[columns]
    live_slots = jnp.arange(A_SLOTS, dtype=jnp.int32)[None, :] < counts[:, None]
    values = jnp.where(live_slots[:, :, None], reached, COARSE).reshape(SLABS, SLAB_BRICKS * A_SLOTS * 2)
    ordered = jnp.sort(values, axis=1)
    repeat = ordered[:, 1:] == ordered[:, :-1]
    cleaned = jnp.concatenate([ordered[:, :1], jnp.where(repeat, COARSE, ordered[:, 1:])], axis=1)
    distinct = jnp.sort(cleaned, axis=1)[:, :PATTERN]
    distinct = jnp.where(distinct == COARSE, -1, distinct)
    owners = PATTERN // PATTERN_OWN
    pattern = distinct.reshape(SLABS, PATTERN_OWN, owners).transpose(0, 2, 1).reshape(SLABS, PATTERN)
    return (columns, counts, targets, pattern.astype(jnp.int32))


def draw_fine_columns(key, part):
    return layout(key)[0]


def draw_fine_counts(key, part):
    return layout(key)[1]


def draw_prolong_columns(key, part):
    return layout(key)[2]


def draw_coarse_pattern(key, part):
    return layout(key)[3]


def steps_of(rng, shape, cuts, least, high):
    factor_of, own = 1.0, jax.random.fold_in(rng, 6)
    for axis_at, shards_of in cuts:
        steps = jnp.exp(jax.random.uniform(jax.random.fold_in(own, axis_at), (shards_of,), jnp.float32, least / len(cuts), high / len(cuts)))
        factor_of = factor_of * jnp.repeat(steps, shape[axis_at] // shards_of).reshape([-1 if axis == axis_at else 1 for axis in range(len(shape))])
    return factor_of


def bell_draw(own_key, dims, deviation, most, cuts=(), kind=jnp.bfloat16):
    values = deviation * jax.random.normal(own_key, dims, jnp.float32)
    if cuts:
        values = values * steps_of(own_key, dims, cuts, -0.22, 0.18)
    return jnp.clip(values, -most, most).astype(kind)


def setup_inputs(seed: int = 0) -> dict:
    splits = jax.random.split(jax.random.key(seed), 8)
    fine_matrix = bell_draw(splits[0], (FINE * BRICK, A_SLOTS * BRICK), BRICK ** -0.5, 0.75, ((0, 192), (1, 4)))
    fine_columns = draw_fine_columns(jax.random.fold_in(splits[7], 71), 0)
    fine_counts = draw_fine_counts(jax.random.fold_in(splits[7], 71), 0)
    prolong = bell_draw(splits[3], (FINE * BRICK, P_SLOTS * BRICK), 1.0, 6.0, ((0, 192),))
    prolong_columns = draw_prolong_columns(jax.random.fold_in(splits[7], 71), 0)
    restrict_rows = bell_draw(splits[5], (COARSE * BRICK, SLAB_BRICKS * BRICK), (SLAB_BRICKS * BRICK) ** -0.5, 0.375, ((0, 192),))
    coarse_pattern = draw_coarse_pattern(jax.random.fold_in(splits[7], 71), 0)
    return dict(fine_matrix=fine_matrix, fine_columns=fine_columns, fine_counts=fine_counts, prolong=prolong, prolong_columns=prolong_columns, restrict_rows=restrict_rows, coarse_pattern=coarse_pattern)


def reference(fine_matrix, fine_columns, fine_counts, prolong, prolong_columns, restrict_rows, coarse_pattern):
    blocks = prolong.reshape(FINE, BRICK, P_SLOTS * BRICK)
    coarse_rows = (SLAB_BRICKS // 2) * BRICK

    def one_slab(slab_index):
        first_row = (slab_index * SLAB_BRICKS).astype(jnp.int32)
        columns = lax.dynamic_slice_in_dim(fine_columns, first_row, SLAB_BRICKS, 0)
        counts = lax.dynamic_slice_in_dim(fine_counts, first_row, SLAB_BRICKS, 0)
        a_rows = lax.dynamic_slice_in_dim(fine_matrix, (first_row * BRICK).astype(jnp.int32), SLAB_BRICKS * BRICK, 0)
        r_rows = lax.dynamic_slice_in_dim(restrict_rows, (slab_index * coarse_rows).astype(jnp.int32), coarse_rows, 0)
        pattern = lax.dynamic_slice_in_dim(coarse_pattern, slab_index.astype(jnp.int32), 1, 0)[0]
        chosen = jnp.take(blocks, columns, axis=0)
        reached = jnp.take(prolong_columns, columns, axis=0)
        live_slots = jnp.arange(A_SLOTS, dtype=jnp.int32)[None, :] < counts[:, None]
        a_blocks = a_rows.reshape(SLAB_BRICKS, BRICK, A_SLOTS, BRICK).astype(jnp.float32)
        products = jnp.einsum('iakb,ikbc->ikac', a_blocks, chosen.astype(jnp.float32), precision=lax.Precision.HIGHEST)
        products = products.reshape(SLAB_BRICKS, A_SLOTS, BRICK, P_SLOTS, BRICK)
        matches = ((reached[:, :, :, None] == pattern[None, None, None, :]) & live_slots[:, :, None, None]).astype(jnp.float32)
        partial_value = jnp.einsum('ikqs,ikaqc->iasc', matches, products, precision=lax.Precision.HIGHEST)
        partial_value = partial_value.reshape(SLAB_BRICKS * BRICK, PATTERN * BRICK)
        return jnp.dot(r_rows.astype(jnp.float32), partial_value, precision=lax.Precision.HIGHEST)

    stacked = lax.map(one_slab, jnp.arange(SLABS, dtype=jnp.int32))
    return stacked.reshape(SLABS * coarse_rows, PATTERN * BRICK)
```

```python
import functools

import jax
import jax.numpy as jnp
from jax import lax
from jax.experimental import pallas as pl
from jax.experimental.pallas import tpu as pltpu
from jax.sharding import PartitionSpec as P

BRICK = 64
A_SLOTS = 24
COLS = 4
SLICE = BRICK // COLS
NEAR_SLOTS = 16
FAR_SLOTS = 16
OWN_BASE = NEAR_SLOTS + FAR_SLOTS
COLUMN_SLOTS = OWN_BASE + 4
OFFSETS = (-2, -1, 1, 2)
MESH = pl.DeviceIdType.MESH


def left_slot(step):
    return 2 * step - 1 if step else 0


def right_slot(step):
    return 2 * step


def ring_slot(distance, size):
    half = size // 2
    return jnp.where(
        distance == 0,
        0,
        jnp.where(distance <= half, 2 * distance - 1, 2 * (size - distance)),
    )


def gather_kernel(
    depth_z,
    depth_y,
    columns,
    counts,
    brick_ids,
    a_hbm,
    p_ref,
    slots,
    a_all,
    halo,
    ids_out,
    buf_a,
    buf_b,
    buf_i,
    send_sem,
    recv_sem,
    local_sem,
):
    slabs = depth_z * depth_y * 2
    fine = slabs * 4
    row = lax.axis_index("row")
    col = lax.axis_index("col")
    core = row % 2
    y = (row // 2) % depth_y
    z = row // (2 * depth_y)

    def at(zz, yy, cc):
        return {"row": (zz * depth_y + yy) * 2 + cc, "col": col}

    y_plus = at(z, (y + 1) % depth_y, core)
    y_minus = at(z, (y + depth_y - 1) % depth_y, core)
    z_plus = at((z + 1) % depth_z, y, core)
    z_minus = at((z + depth_z - 1) % depth_z, y, core)
    partner = at(z, y, 1 - core)
    halo_peers = [{"row": (row + o + slabs) % slabs, "col": col} for o in OFFSETS]
    x_peers = [{"row": row, "col": (col + o) % COLS} for o in (1, 2, 3)]

    barrier = pltpu.get_barrier_semaphore()
    peers = [y_plus, y_minus, z_plus, z_minus, partner] + halo_peers + x_peers
    for peer in peers:
        pl.semaphore_signal(barrier, inc=1, device_id=peer, device_id_type=MESH)

    rows = pl.ds(pl.multiple_of(col * SLICE, SLICE), SLICE)
    own_copies = [
        pltpu.make_async_copy(p_ref.at[0:2, rows, :], buf_a.at[0:2], local_sem.at[0]),
        pltpu.make_async_copy(p_ref.at[2:4, rows, :], buf_b.at[0:2], local_sem.at[1]),
        pltpu.make_async_copy(a_hbm, a_all.at[col], local_sem.at[2]),
    ]
    for copy in own_copies:
        copy.start()
    lane = lax.broadcasted_iota(jnp.int32, (1, 128), 1)
    id_row = jnp.zeros((1, 128), jnp.int32)
    for i in range(4):
        for q in range(2):
            id_row = jnp.where(lane == 2 * i + q, brick_ids[i, q], id_row)
    buf_i[0] = id_row
    own_copies[0].wait()
    own_copies[1].wait()
    pl.semaphore_wait(barrier, len(peers))

    started = []
    events = []
    done = set()
    table = {}

    def message(name, time, needs, src, dst, device):
        index = len(events)
        copy = pltpu.make_async_remote_copy(
            src_ref=src,
            dst_ref=dst,
            send_sem=send_sem.at[index],
            recv_sem=recv_sem.at[index],
            device_id=device,
            device_id_type=MESH,
        )
        table[name] = copy
        events.append((time, index, tuple(needs), copy))

    hop = 1.7

    def line(tag, buf, width, size, plus, minus):
        for step in range(1, size // 2 + 1):
            for way, device, slot, last in (
                ("L", plus, left_slot, size // 2),
                ("R", minus, right_slot, (size - 1) // 2),
            ):
                if step > last:
                    continue
                message(
                    (tag, "line", way, step),
                    hop * (step - 1),
                    [(tag, "line", way, step - 1)] if step > 1 else [],
                    buf.at[pl.ds(width * slot(step - 1), width)],
                    buf.at[pl.ds(width * slot(step), width)],
                    device,
                )

    def line_needs(tag, size, lo, hi):
        names, depth = [], 0
        for way, slot, last in (("L", left_slot, size // 2), ("R", right_slot, (size - 1) // 2)):
            for step in range(1, last + 1):
                if lo <= slot(step) < hi:
                    names.append((tag, "line", way, step))
                    depth = max(depth, step)
        return names, depth

    def ring(tag, buf, width, inner, size, pieces, plus, minus, pace):
        half = size // 2
        for step in range(1, half + 1):
            for way, device, slot in (("L", plus, left_slot), ("R", minus, right_slot)):
                for at_piece, (lo, hi) in enumerate(pieces):
                    target = slot(step)
                    if step == half and size % 2 == 0:
                        mine = at_piece < (len(pieces) + 1) // 2
                        if mine != (way == "L"):
                            continue
                        target = size - 1
                    names, depth = line_needs(tag, inner, lo, hi)
                    if step > 1:
                        names = [(tag, "ring", way, step - 1, at_piece)]
                    message(
                        (tag, "ring", way, step, at_piece),
                        hop * depth + pace * (step - 1),
                        names,
                        buf.at[pl.ds(width * (slot(step - 1) * inner + lo), width * (hi - lo))],
                        buf.at[pl.ds(width * (target * inner + lo), width * (hi - lo))],
                        device,
                    )

    def forward(tag, buf, width, inner, size, pieces, pace, groups):
        total = width * inner * size
        for lo, hi in groups:
            needs, when = [], 0.0
            names, depth = line_needs(tag, inner, 0, inner)
            for chunk in range(lo, hi):
                if chunk == 0:
                    needs += names
                    when = max(when, hop * depth)
                    continue
                step = (chunk + 1) // 2
                for at_piece in range(len(pieces)):
                    if chunk == size - 1 and size % 2 == 0:
                        way = "L" if at_piece < (len(pieces) + 1) // 2 else "R"
                    else:
                        way = "L" if chunk % 2 else "R"
                    needs.append((tag, "ring", way, step, at_piece))
                when = max(when, hop * depth + pace * step)
            span = width * inner
            message(
                (tag, "forward", lo),
                when + 0.1,
                needs,
                buf.at[pl.ds(span * lo, span * (hi - lo))],
                buf.at[pl.ds(total + span * lo, span * (hi - lo))],
                partner,
            )

    def pairs(size):
        groups = [(0, 1)] + [(k, min(k + 2, size)) for k in range(1, size, 2)]
        return groups

    def cut(count):
        return [(0, count // 2), (count // 2, count)]

    line("a", buf_a, 2, depth_y, y_plus, y_minus)
    line("b", buf_b, 2, depth_z, z_plus, z_minus)
    line("i", buf_i, 1, depth_y, y_plus, y_minus)
    for at_offset, (o, peer) in enumerate(zip(OFFSETS, halo_peers)):
        lands = 3 - at_offset
        message(
            ("halo", at_offset),
            0.05,
            [],
            p_ref.at[:, rows, :],
            halo.at[col, pl.ds(4 * lands, 4)],
            peer,
        )
    halo_names = [("halo", k) for k in range(4)]
    for k, peer in enumerate(x_peers):
        message(
            ("near", k), 4.0, halo_names, halo.at[col, 0:NEAR_SLOTS], halo.at[col, 0:NEAR_SLOTS], peer
        )
        message(("share", k), 0.1, [], a_hbm, a_all.at[col], peer)
    ring("a", buf_a, 2, depth_y, depth_z, cut(depth_y), z_plus, z_minus, 2.0)
    ring("b", buf_b, 2, depth_z, depth_y, cut(depth_z), y_plus, y_minus, 2.4)
    ring("i", buf_i, 1, depth_y, depth_z, [(0, depth_y)], z_plus, z_minus, 2.0)
    forward("a", buf_a, 2, depth_y, depth_z, cut(depth_y), 2.0, pairs(depth_z))
    forward("b", buf_b, 2, depth_z, depth_y, cut(depth_z), 2.4, pairs(depth_y))
    forward("i", buf_i, 1, depth_y, depth_z, [(0, depth_y)], 2.0, [(0, depth_z)])

    def await_all(names):
        for name in names:
            if name not in done:
                done.add(name)
                table[name].wait_recv()

    def decode():
        found = []
        for i in range(4):

            def body(k, carry, i=i):
                count, picks = carry[0], carry[1:]
                j = columns[i, k]
                distance = lax.rem(j - 4 * row + 8 + fine, fine)
                is_far = distance >= 20
                brick = jnp.where(
                    distance < 8,
                    distance,
                    jnp.where(distance < 12, distance - 8 + OWN_BASE, distance - 4),
                )
                place = NEAR_SLOTS + 4 * i + jnp.minimum(count, 3)
                slot = jnp.where(is_far, place, brick)
                slots[i, k] = jnp.where(k < counts[i], slot, COLUMN_SLOTS)
                picks = tuple(
                    jnp.where(is_far & (count == m), j, picks[m]) for m in range(4)
                )
                return (count + is_far.astype(jnp.int32),) + picks

            zero = jnp.int32(0)
            carry = lax.fori_loop(0, A_SLOTS, body, (zero,) * 5)
            found += list(carry[1:])
        return found

    ordered = sorted(events, key=lambda e: (e[0], e[1]))
    far = None
    for time, index, needs, copy in ordered:
        if far is None and time > 0.2:
            far = decode()
        await_all(needs)
        copy.start()
        started.append(copy)

    def place_of(slab):
        other = slab % 2
        yy = (slab // 2) % depth_y
        zz = slab // (2 * depth_y)
        apart_z = lax.rem(z - zz + depth_z, depth_z)
        apart_y = lax.rem(y - yy + depth_y, depth_y)
        side = jnp.where(other == core, 0, 1)
        slot_z = ring_slot(apart_z, depth_z)
        slot_y = ring_slot(apart_y, depth_y)
        first = (side * depth_z + slot_z) * depth_y + slot_y
        second = (side * depth_y + slot_y) * depth_z + slot_z
        return first, second

    for name in list(table):
        if name[0] in "abi":
            await_all([name])
    for f in range(FAR_SLOTS):
        slab, i = far[f] // 4, far[f] % 4
        first, second = place_of(slab)
        low = buf_a[2 * first + i % 2]
        high = buf_b[2 * second + i % 2]
        halo[col, NEAR_SLOTS + f] = jnp.where(i < 2, low, high)
        ids_out[NEAR_SLOTS + f] = jnp.where(lane // 2 == i, buf_i[first], 0)
    await_all([("near", k) for k in range(3)])
    last = []
    base = len(events)
    for k, peer in enumerate(x_peers):
        copy = pltpu.make_async_remote_copy(
            src_ref=halo.at[col, pl.ds(NEAR_SLOTS, FAR_SLOTS)],
            dst_ref=halo.at[col, pl.ds(NEAR_SLOTS, FAR_SLOTS)],
            send_sem=send_sem.at[base + k],
            recv_sem=recv_sem.at[base + k],
            device_id=peer,
            device_id_type=MESH,
        )
        copy.start()
        last.append(copy)
    for at_offset, o in enumerate(OFFSETS):
        first, _ = place_of(lax.rem(row + o + slabs, slabs))
        for i in range(4):
            ids_out[4 * at_offset + i] = jnp.where(lane // 2 == i, buf_i[first], 0)
    for i in range(4):
        ids_out[OWN_BASE + i] = jnp.where(lane // 2 == i, id_row, 0)
    await_all([("share", k) for k in range(3)])
    own_copies[2].wait()
    for copy in started:
        copy.wait_send()
    for copy in last:
        copy.wait()


def message_count(depth_z, depth_y):
    def pieces(size):
        return 2 * (2 * (size // 2 - 1)) + 2

    lines = 2 * (depth_y - 1) + (depth_z - 1)
    rings = pieces(depth_z) + pieces(depth_y) + depth_z - 1
    forwards = (depth_z // 2 + 1) + (depth_y // 2 + 1) + 1
    return lines + rings + forwards + 4 + 3 + 3 + 3


def compute_kernel(
    slots, pattern, a_all, halo, p_ref, ids, restrict, out, acc, masks, lhs, weights
):
    col = lax.axis_index("col")
    width = out.shape[1]
    share = a_all.shape[2] // BRICK
    acc[...] = jnp.zeros_like(acc)
    for i in range(4):
        r_part = restrict[:, BRICK * i : BRICK * (i + 1)]
        for x in range(COLS):
            t = lax.dot_general(
                a_all[x, BRICK * i : BRICK * (i + 1), :],
                r_part,
                (((0,), (1,)), ((), ())),
                preferred_element_type=jnp.float32,
            )
            for k in range(share):
                slot = slots[i, share * x + k]
                acc[slot] = acc[slot] + t[BRICK * k : BRICK * (k + 1), :]

    lane = lax.broadcasted_iota(jnp.int32, (1, 128), 1)
    low_half = lane < BRICK
    id_rows = ids[...]
    for q in range(2):
        kept = jnp.where((lane % 2 == q)[None], id_rows, 0)
        names = jnp.sum(kept.astype(jnp.float32), axis=2, keepdims=True).astype(jnp.int32)
        for pair in range(width // 128):
            first = pattern[0, col * (width // BRICK) + 2 * pair]
            second = pattern[0, col * (width // BRICK) + 2 * pair + 1]
            wanted = jnp.where(low_half, first, second)
            masks[q, :, :, 128 * pair : 128 * (pair + 1)] = (names == wanted[None]).astype(jnp.float32)

    def place(c, x, piece):
        wide = piece.astype(jnp.float32)
        turned = pltpu.roll(wide, BRICK, 1)
        for q in range(2):
            both = jnp.where(low_half, wide, turned) if q == 0 else jnp.where(low_half, turned, wide)
            for pair in range(width // 128):
                lanes = slice(128 * pair, 128 * (pair + 1))
                mask = masks[q, c, :, lanes]
                weights[q, c, SLICE * x : SLICE * (x + 1), lanes] = (both * mask).astype(
                    jnp.bfloat16
                )

    def spread(c, _):
        for x in range(COLS):
            place(c, x, halo[x, c])
        return 0

    lax.fori_loop(0, OWN_BASE, spread, 0)

    def spread_own(i, _):
        for x in range(COLS):
            place(OWN_BASE + i, x, p_ref[i, SLICE * x : SLICE * (x + 1), :])
        return 0

    lax.fori_loop(0, 4, spread_own, 0)

    depth = COLUMN_SLOTS * BRICK
    turned = jnp.transpose(acc[0:COLUMN_SLOTS].reshape(depth, 128))
    high = turned.astype(jnp.bfloat16)
    lhs[0:128, :] = high
    lhs[128:256, :] = (turned - high.astype(jnp.float32)).astype(jnp.bfloat16)
    total = jnp.dot(
        lhs[...], weights[0].reshape(depth, width), preferred_element_type=jnp.float32
    ) + jnp.dot(lhs[...], weights[1].reshape(depth, width), preferred_element_type=jnp.float32)
    out[...] = total[0:128] + total[128:256]


def build(mesh, depth_z, depth_y):
    vmem = pl.BlockSpec(memory_space=pltpu.VMEM)
    smem = pl.BlockSpec(memory_space=pltpu.SMEM)
    anywhere = pl.BlockSpec(memory_space=pl.ANY)

    def local(
        fine_matrix, fine_columns, fine_counts, prolong, prolong_columns, restrict_rows, coarse_pattern
    ):
        blocks = prolong.reshape(4, BRICK, 128)
        share = fine_matrix.shape[1]
        devices = depth_z * depth_y * 2
        count = message_count(depth_z, depth_y)
        slots, a_all, halo, ids = pl.pallas_call(
            functools.partial(gather_kernel, depth_z, depth_y),
            name="exchange",
            out_shape=(
                jax.ShapeDtypeStruct((4, A_SLOTS), jnp.int32),
                jax.ShapeDtypeStruct((COLS, 256, share), jnp.bfloat16),
                jax.ShapeDtypeStruct((COLS, OWN_BASE, SLICE, 128), jnp.bfloat16),
                jax.ShapeDtypeStruct((COLUMN_SLOTS, 1, 128), jnp.int32),
            ),
            in_specs=[smem, smem, smem, anywhere, vmem],
            out_specs=(smem, vmem, vmem, vmem),
            scratch_shapes=[
                pltpu.VMEM((2 * devices, SLICE, 128), jnp.bfloat16),
                pltpu.VMEM((2 * devices, SLICE, 128), jnp.bfloat16),
                pltpu.VMEM((devices, 1, 128), jnp.int32),
                pltpu.SemaphoreType.DMA((count,)),
                pltpu.SemaphoreType.DMA((count,)),
                pltpu.SemaphoreType.DMA((3,)),
            ],
            compiler_params=pltpu.CompilerParams(collective_id=0, has_side_effects=True),
        )(fine_columns, fine_counts, prolong_columns, fine_matrix, blocks)
        width = coarse_pattern.shape[1] * BRICK // COLS
        return pl.pallas_call(
            compute_kernel,
            name="assemble",
            out_shape=jax.ShapeDtypeStruct((128, width), jnp.float32),
            in_specs=[smem, smem, vmem, vmem, vmem, vmem, vmem],
            out_specs=vmem,
            scratch_shapes=[
                pltpu.VMEM((COLUMN_SLOTS + 1, BRICK, 128), jnp.float32),
                pltpu.VMEM((2, COLUMN_SLOTS, 1, width), jnp.float32),
                pltpu.VMEM((256, COLUMN_SLOTS * BRICK), jnp.bfloat16),
                pltpu.VMEM((2, COLUMN_SLOTS, BRICK, width), jnp.bfloat16),
            ],
        )(slots, coarse_pattern, a_all, halo, blocks, ids, restrict_rows)

    return jax.shard_map(
        local,
        mesh=mesh,
        in_specs=(
            P("row", "col"),
            P("row", None),
            P("row"),
            P("row", None),
            P("row", None),
            P("row", None),
            P("row", None),
        ),
        out_specs=P("row", "col"),
        check_vma=False,
    )


def solution(mesh):
    return build(mesh, 12, 8)
```
